256 devices in a mesh: seq: 64 (over y, z, core), tp: 4 (over x).
Axes of the slice: x: 4, y: 4, z: 8, core: 2. Of those that a mesh axis runs over, the one named last changes fastest.
Arguments:
- normed_input: bfloat16 [32768, 5376], P('seq', 'tp'), may hold values from -6 to 6
- query: bfloat16 [32768, 4096], P('seq', 'tp'), may hold values from -220 to 220, as said below
- key: bfloat16 [32768, 2048], P('seq', 'tp'), may hold values from -7 to 7
- value: bfloat16 [32768, 2048], P('seq', 'tp'), may hold values from -6 to 6
- adapter_down_maps: bfloat16 [64, 16, 5376], P(None, None, 'tp'), may hold values from -0.078125 to 0.078125
- adapter_up_maps: bfloat16 [64, 16, 2048], P(None, None, 'tp'), may hold values from -1.5 to 1.5
- block_adapter_choice: int32 [16], replicated, may hold values from 0 to 63
Outputs:
- attended: bfloat16 [32768, 4096], P('seq', 'tp')
The draws below stay inside these ranges and needn't reach their ends.
Inputs may be any that keep to these rules, and one draw needn't show every extreme that they name: `query`: queries; some may be aligned with nearby keys.
All inputs are finite; a program needn't handle non-finite values.
Results may differ from the reference program's by a relative error of at most 0.014.
Values may be sent and summed in bfloat16 or wider, within the bound.
A program may use at most 128 MiB of HBM per device.

```python
import math
import jax
import jax.numpy as jnp
import numpy as np
from jax import lax

MODEL_WIDTH = 5376
HEADS = 32
KEY_VALUE_HEADS = 16
HEAD_WIDTH = 128
WINDOW = 1024
ADAPTER_COUNT = 64
ADAPTER_RANK = 16
SEG_LEN = 2048
TOKENS = 32768
SEGMENTS = 16


def query_key_pair(key):
    base = jax.random.fold_in(key, 11)
    key_k, key_q = jax.random.split(base, 2)
    keys_drawn = jnp.clip(jax.random.normal(key_k, (TOKENS, KEY_VALUE_HEADS * HEAD_WIDTH), jnp.float32), -6.0, 6.0)
    queries = jnp.clip(jax.random.normal(key_q, (TOKENS, HEADS, HEAD_WIDTH), jnp.float32), -6.0, 6.0)
    return (queries.reshape(TOKENS, HEADS * HEAD_WIDTH), keys_drawn)


def draw_query(key, part):
    return query_key_pair(key)[0].astype(jnp.bfloat16)


def draw_key(key, part):
    return query_key_pair(key)[1].astype(jnp.bfloat16)


def touch_ends(values, own_key, low, largest):
    longest = values.shape.index(max(values.shape))
    spots = []
    for shift in (0, 1):
        where = [jax.random.randint(jax.random.fold_in(own_key, axis), (), 0, length) for axis, length in enumerate(values.shape)]
        where[longest] = (where[longest] + shift) % values.shape[longest]
        spots.append(tuple(where))
    return values.at[spots[0]].set(low).at[spots[1]].set(largest)


def block_scale(stream_key, shape, shards, smallest, high):
    gain = 1.0
    for position, shards_of in shards:
        heights = jax.random.uniform(jax.random.fold_in(jax.random.fold_in(stream_key, 6), position), (shards_of,), jnp.float32, smallest / len(shards), high / len(shards))
        gain = gain * jnp.repeat(jnp.exp(heights), shape[position] // shards_of).reshape((-1,) + (1,) * (len(shape) - 1 - position))
    return gain


def rank_table(number_of, lean):
    loads = [(1 << 20) // math.isqrt(rank ** lean) + 1 for rank in range(1, number_of + 1)]
    width = 1 + sum(loads) // (1 << 30)
    return np.cumsum(np.array([max(1, weight // width) for weight in loads]))


def skewed_ids(own_key, shape, number_of, skew):
    table = rank_table(number_of, skew)
    ticket = jax.random.randint(jax.random.fold_in(own_key, 1), shape, 0, int(table[number_of - 1]))
    rank = jnp.searchsorted(jnp.asarray(table, jnp.int32), ticket, side="right")
    return jax.random.permutation(jax.random.fold_in(own_key, 2), number_of)[rank].astype(jnp.int32)


def scatter_about(key, shape, width, most, cuts=(), held_as=jnp.bfloat16):
    array = width * jax.random.normal(key, shape, jnp.float32)
    if cuts:
        array = array * block_scale(key, shape, cuts, -0.22, 0.18)
    return jnp.clip(array, -most, most).astype(held_as)


def setup_inputs(seed: int = 0) -> dict:
    key_list = jax.random.split(jax.random.key(seed), 8)
    normed_input = scatter_about(key_list[0], (TOKENS, MODEL_WIDTH), 1.0, 6.0, ((0, 64), (1, 4)))
    query = draw_query(jax.random.fold_in(key_list[7], 71), 0)
    key = draw_key(jax.random.fold_in(key_list[7], 71), 0)
    value = scatter_about(key_list[3], (TOKENS, KEY_VALUE_HEADS * HEAD_WIDTH), 1.0, 6.0, ((0, 64), (1, 4)))
    adapter_down_maps = scatter_about(key_list[4], (ADAPTER_COUNT, ADAPTER_RANK, MODEL_WIDTH), MODEL_WIDTH ** -0.5, 0.078125, ((2, 4),))
    adapter_up_maps = scatter_about(key_list[5], (ADAPTER_COUNT, ADAPTER_RANK, KEY_VALUE_HEADS * HEAD_WIDTH), ADAPTER_RANK ** -0.5, 1.5, ((2, 4),))
    block_adapter_choice = touch_ends(skewed_ids(key_list[6], (SEGMENTS,), ADAPTER_COUNT, 2), jax.random.fold_in(key_list[6], 3), 0, ADAPTER_COUNT - 1).astype(jnp.int32)
    return {"normed_input": normed_input, "query": query, "key": key, "value": value, "adapter_down_maps": adapter_down_maps, "adapter_up_maps": adapter_up_maps, "block_adapter_choice": block_adapter_choice}


query_scale = 168.0 ** -0.5


def reference(normed_input, query, key, value, adapter_down_maps, adapter_up_maps, block_adapter_choice):
    nseg = block_adapter_choice.shape[0]
    columns = value.shape[1]

    def segment_values(seg):
        first = (seg * SEG_LEN).astype(jnp.int32)
        token_rows = lax.dynamic_slice_in_dim(normed_input, first, SEG_LEN, 0)
        adapter_index = block_adapter_choice[seg]
        rank_activation = jnp.dot(token_rows, adapter_down_maps[adapter_index].T, preferred_element_type=jnp.float32).astype(jnp.bfloat16)
        base = lax.dynamic_slice_in_dim(value, first, SEG_LEN, 0)
        value_update = jnp.dot(rank_activation, adapter_up_maps[adapter_index], preferred_element_type=jnp.float32)
        return (base.astype(jnp.float32) + value_update).astype(jnp.bfloat16)

    value_full = lax.map(segment_values, jnp.arange(nseg, dtype=jnp.int32)).reshape(TOKENS, columns)
    group = HEADS // KEY_VALUE_HEADS
    qblock = min(512, TOKENS)
    span = qblock + WINDOW
    key_pad = jnp.concatenate([jnp.zeros((WINDOW, columns), jnp.bfloat16), key], axis=0)
    val_pad = jnp.concatenate([jnp.zeros((WINDOW, columns), jnp.bfloat16), value_full], axis=0)

    def one_block(blk):
        first = (blk * qblock).astype(jnp.int32)
        qrows = lax.dynamic_slice_in_dim(query, first, qblock, 0).astype(jnp.float32)
        qrows = qrows.reshape(qblock, KEY_VALUE_HEADS, group, HEAD_WIDTH)
        krows = lax.dynamic_slice_in_dim(key_pad, first, span, 0).astype(jnp.float32).reshape(span, KEY_VALUE_HEADS, HEAD_WIDTH)
        vrows = lax.dynamic_slice_in_dim(val_pad, first, span, 0).astype(jnp.float32).reshape(span, KEY_VALUE_HEADS, HEAD_WIDTH)
        scores = jnp.einsum("qkgd,lkd->kgql", qrows, krows) * query_scale
        qpos = first + jnp.arange(qblock, dtype=jnp.int32)[:, None]
        kpos = first - WINDOW + jnp.arange(span, dtype=jnp.int32)[None, :]
        usable = (kpos <= qpos) & (qpos - kpos < WINDOW) & (kpos >= 0)
        scores = jnp.where(usable, scores, -1e30)
        top = jnp.max(scores, axis=-1, keepdims=True)
        expo = jnp.exp(scores - top)
        weights = (expo / jnp.sum(expo, axis=-1, keepdims=True)).astype(jnp.bfloat16)
        out = jnp.einsum("kgql,lkd->qkgd", weights.astype(jnp.float32), vrows)
        return out.astype(jnp.bfloat16).reshape(qblock, HEADS * HEAD_WIDTH)

    blocks = lax.map(one_block, jnp.arange(TOKENS // qblock, dtype=jnp.int32))
    return blocks.reshape(TOKENS, HEADS * HEAD_WIDTH)
```

```python
import functools

import jax
import jax.numpy as jnp
from jax import lax
from jax.experimental import pallas as pl
from jax.experimental.pallas import tpu as pltpu
from jax.sharding import PartitionSpec as P

HEAD_WIDTH = 128
SEG_LEN = 2048
MESH = pl.DeviceIdType.MESH
EARLY = 3
SCALE2 = 168.0 ** (-0.5) * 1.4426950408889634
NEG = -1e30
BIG = 1e30


def kernel(
    n_seq, n_tp,
    choice_ref, x_ref, q_ref, k_ref, v_ref, down_ref, up_ref,
    out_ref,
    x_v, down_v, up_v, q_v, kall, vraw, vf, lat, latall, upsel, out_v,
    in_sem, kv_sem, out_sem,
    ring_send, ring_recv, pair_send, pair_recv,
    part_send, part_recv, lat_send, lat_recv,
):
    me = lax.axis_index("seq")
    tp = lax.axis_index("tp")
    core = lax.rem(me, 2)
    tok = q_ref.shape[0]
    kv = k_ref.shape[1] // HEAD_WIDTH
    half = tok // 2
    span = 2 * tok + half

    def seq_at(step):
        return lax.rem(me + n_seq + step, n_seq)

    barrier = pltpu.get_barrier_semaphore()
    for step in (1, 2, -1, -2):
        pl.semaphore_signal(barrier, inc=1, device_id=(seq_at(step), tp), device_id_type=MESH)
    for step in range(1, n_tp):
        pl.semaphore_signal(
            barrier, inc=1, device_id=(me, lax.rem(tp + step, n_tp)), device_id_type=MESH
        )

    loads = [
        pltpu.make_async_copy(x_ref, x_v, in_sem.at[0]),
        pltpu.make_async_copy(down_ref, down_v, in_sem.at[1]),
        pltpu.make_async_copy(up_ref, up_v, in_sem.at[2]),
        pltpu.make_async_copy(q_ref, q_v, in_sem.at[3]),
    ]
    for load in loads:
        load.start()

    def columns(head):
        return pl.ds(pl.multiple_of(head * HEAD_WIDTH, HEAD_WIDTH), HEAD_WIDTH)

    def own_copy(which, head):
        src = (k_ref, v_ref)[which].at[:, columns(head)]
        dst = (kall, vraw)[which].at[head, pl.ds(2 * tok, tok), :]
        return pltpu.make_async_copy(src, dst, kv_sem.at[which, head])

    for head in range(kv):
        own_copy(0, head).start()
        own_copy(1, head).start()

    def ring_copy(which, head):
        return pltpu.make_async_remote_copy(
            src_ref=(k_ref, v_ref)[which].at[:, columns(head)],
            dst_ref=(kall, vraw)[which].at[head, pl.ds(0, tok), :],
            send_sem=ring_send.at[which, head],
            recv_sem=ring_recv.at[which, head],
            device_id=(seq_at(2), tp),
            device_id_type=MESH,
        )

    def give_copy(which, head):
        return pltpu.make_async_remote_copy(
            src_ref=(k_ref, v_ref)[which].at[:, columns(head)],
            dst_ref=(kall, vraw)[which].at[head, pl.ds(tok, tok), :],
            send_sem=pair_send.at[which, head],
            recv_sem=pair_recv.at[which, head],
            device_id=(seq_at(1), tp),
            device_id_type=MESH,
        )

    def relay_copy(which, head):
        buffer = (kall, vraw)[which]
        return pltpu.make_async_remote_copy(
            src_ref=buffer.at[head, pl.ds(0, tok), :],
            dst_ref=buffer.at[head, pl.ds(tok, tok), :],
            send_sem=pair_send.at[which, head],
            recv_sem=pair_recv.at[which, head],
            device_id=(seq_at(-1), tp),
            device_id_type=MESH,
        )

    pl.semaphore_wait(barrier, 4 + n_tp - 1)

    order = [(which, head) for head in range(kv) for which in range(2)]
    for which, head in order[:EARLY]:
        ring_copy(which, head).start()

    @pl.when(core == 0)
    def _():
        for which, head in order:
            give_copy(which, head).start()

    loads[0].wait()
    loads[1].wait()
    chip_seg = (me * tok) // SEG_LEN
    lat[tp] = jnp.dot(
        down_v[choice_ref[chip_seg]], x_v[...], preferred_element_type=jnp.float32
    )

    def part_copy(step):
        return pltpu.make_async_remote_copy(
            src_ref=lat.at[tp],
            dst_ref=lat.at[tp],
            send_sem=part_send.at[step - 1],
            recv_sem=part_recv.at[step - 1],
            device_id=(me, lax.rem(tp + step, n_tp)),
            device_id_type=MESH,
        )

    def part_arrival(step):
        slot = lat.at[lax.rem(tp + n_tp - step, n_tp)]
        return pltpu.make_async_remote_copy(
            src_ref=slot,
            dst_ref=slot,
            send_sem=part_send.at[step - 1],
            recv_sem=part_recv.at[step - 1],
            device_id=(me, lax.rem(tp + step, n_tp)),
            device_id_type=MESH,
        )

    for step in range(1, n_tp):
        part_copy(step).start()

    loads[2].wait()
    for source in range(3):
        segment = (seq_at(source - 2) * tok) // SEG_LEN
        upsel[source] = up_v[choice_ref[segment]]

    for step in range(1, n_tp):
        part_arrival(step).wait_recv()
    total = lat[0]
    for step in range(1, n_tp):
        total = total + lat[step]
    latall[2] = total.astype(jnp.bfloat16)

    def lat_copy(step):
        return pltpu.make_async_remote_copy(
            src_ref=latall.at[2],
            dst_ref=latall.at[2 - step],
            send_sem=lat_send.at[step - 1],
            recv_sem=lat_recv.at[step - 1],
            device_id=(seq_at(step), tp),
            device_id_type=MESH,
        )

    lat_copy(1).start()
    lat_copy(2).start()
    for which, head in order[EARLY:]:
        ring_copy(which, head).start()

    loads[3].wait()
    lat_copy(1).wait_recv()
    lat_copy(2).wait_recv()

    row = lax.broadcasted_iota(jnp.int32, (half, half), 0)
    col = lax.broadcasted_iota(jnp.int32, (half, half), 1)
    later = col > row
    have = [me >= 2, me >= 1, None]

    def one_head(head, carry):
        own_copy(0, head).wait()
        own_copy(1, head).wait()
        ring_copy(0, head).wait_recv()
        ring_copy(1, head).wait_recv()

        @pl.when(core == 1)
        def _():
            relay_copy(0, head).start()
            relay_copy(1, head).start()

        give_copy(0, head).wait_recv()
        give_copy(1, head).wait_recv()
        for source in range(3):
            rows = pl.ds(source * tok, tok)
            update = lax.dot_general(
                latall[source], upsel[source, :, columns(head)],
                (((0,), (0,)), ((), ())), preferred_element_type=jnp.float32,
            )
            vf[rows, :] = (vraw[head, rows, :].astype(jnp.float32) + update).astype(jnp.bfloat16)

        for block in range(2):
            first = block * half
            keys = kall[head, pl.ds(first, span), :]
            vals = vf[pl.ds(first, span), :]
            edges = [0, 2 * half - first, 4 * half - first, span]
            for member in range(2):
                at = pl.multiple_of((head * 2 + member) * HEAD_WIDTH, HEAD_WIDTH)
                rows = q_v[pl.ds(first, half), pl.ds(at, HEAD_WIDTH)]
                scores = lax.dot_general(
                    rows, keys, (((1,), (1,)), ((), ())), preferred_element_type=jnp.float32
                )
                scores = jnp.concatenate(
                    [
                        jnp.where(later, scores[:, :half], NEG),
                        scores[:, half : span - half],
                        jnp.where(later, NEG, scores[:, span - half :]),
                    ],
                    axis=1,
                )
                top = None
                for source in range(3):
                    part = jnp.max(scores[:, edges[source] : edges[source + 1]], axis=1, keepdims=True)
                    if have[source] is not None:
                        part = jnp.where(have[source], part, NEG)
                    top = part if top is None else jnp.maximum(top, part)
                top = top * SCALE2
                expo = []
                for source in range(3):
                    shift = top if have[source] is None else jnp.where(have[source], top, BIG)
                    expo.append(
                        jnp.exp2(scores[:, edges[source] : edges[source + 1]] * SCALE2 - shift)
                    )
                expo = jnp.concatenate(expo, axis=1)
                norm = jnp.sum(expo, axis=1, keepdims=True)
                out = jnp.dot(expo.astype(jnp.bfloat16), vals, preferred_element_type=jnp.float32)
                out_v[pl.ds(first, half), pl.ds(at, HEAD_WIDTH)] = (out / norm).astype(jnp.bfloat16)
        out_copy(head).start()
        return carry

    def out_copy(head):
        at = pl.ds(pl.multiple_of(head * 2 * HEAD_WIDTH, 2 * HEAD_WIDTH), 2 * HEAD_WIDTH)
        return pltpu.make_async_copy(out_v.at[:, at], out_ref.at[:, at], out_sem.at[head])

    lax.fori_loop(0, kv, one_head, 0)

    for step in range(1, n_tp):
        part_copy(step).wait_send()
    lat_copy(1).wait_send()
    lat_copy(2).wait_send()
    for which, head in order:
        ring_copy(which, head).wait_send()
        give_copy(which, head).wait_send()
    for head in range(kv):
        out_copy(head).wait()


def on_device(
    n_seq, n_tp,
    normed_input, query, key, value, adapter_down_maps, adapter_up_maps, block_adapter_choice,
):
    tok, width = normed_input.shape
    kv = key.shape[1] // HEAD_WIDTH
    count, rank, columns = adapter_up_maps.shape
    bf16 = jnp.bfloat16
    dma = pltpu.SemaphoreType.DMA
    hbm = pl.BlockSpec(memory_space=pl.ANY)
    return pl.pallas_call(
        functools.partial(kernel, n_seq, n_tp),
        out_shape=jax.ShapeDtypeStruct(query.shape, bf16),
        in_specs=[pl.BlockSpec(memory_space=pltpu.SMEM)] + [hbm] * 6,
        out_specs=hbm,
        scratch_shapes=[
            pltpu.VMEM((width, tok), bf16),
            pltpu.VMEM((count, rank, width), bf16),
            pltpu.VMEM((count, rank, columns), bf16),
            pltpu.VMEM(query.shape, bf16),
            pltpu.VMEM((kv, 3 * tok, HEAD_WIDTH), bf16),
            pltpu.VMEM((kv, 3 * tok, HEAD_WIDTH), bf16),
            pltpu.VMEM((3 * tok, HEAD_WIDTH), bf16),
            pltpu.VMEM((n_tp, rank, tok), jnp.float32),
            pltpu.VMEM((3, rank, tok), bf16),
            pltpu.VMEM((3, rank, columns), bf16),
            pltpu.VMEM(query.shape, bf16),
            dma((4,)),
            dma((2, kv)),
            dma((kv,)),
            dma((2, kv)), dma((2, kv)), dma((2, kv)), dma((2, kv)),
            dma((n_tp - 1,)), dma((n_tp - 1,)), dma((2,)), dma((2,)),
        ],
        compiler_params=pltpu.CompilerParams(collective_id=0, has_side_effects=True),
    )(
        block_adapter_choice, normed_input.T, query, key, value,
        adapter_down_maps, adapter_up_maps,
    )


def solution(mesh):
    placed = (
        P("seq", "tp"),
        P("seq", "tp"),
        P("seq", "tp"),
        P("seq", "tp"),
        P(None, None, "tp"),
        P(None, None, "tp"),
        P(),
    )
    return jax.shard_map(
        functools.partial(on_device, mesh.shape["seq"], mesh.shape["tp"]),
        mesh=mesh, in_specs=placed, out_specs=P("seq", "tp"), check_vma=False,
    )
```

```python
import functools

import jax
import jax.numpy as jnp
from jax import lax
from jax.experimental import pallas as pl
from jax.experimental.pallas import tpu as pltpu
from jax.sharding import PartitionSpec as P

HEAD_WIDTH = 128
SEG_LEN = 2048
MESH = pl.DeviceIdType.MESH
EARLY = 6
SCALE2 = 168.0 ** (-0.5) * 1.4426950408889634
NEG = -1e30
BIG = 1e30
ROW = 16
DETOUR = ((1, 1, 0), (1, 2, 0), (1, 3, 0))


def kernel(
    n_seq, n_tp,
    choice_ref, x_ref, q_ref, k_ref, v_ref, down_ref, up_ref,
    out_ref,
    x_v, down_v, up_v, q_v, kall, vraw, vf, lat, latall, upsel, hold, m_s, l_s, acc_s,
    in_sem, kv_sem,
    ring_send, ring_recv, pair_send, pair_recv,
    part_send, part_recv, lat_send, lat_recv,
    hop_send, hop_recv, fwd_send,
):
    me = lax.axis_index("seq")
    tp = lax.axis_index("tp")
    core = lax.rem(me, 2)
    partner = me + 1 - 2 * core
    place = lax.rem(me, ROW)
    last_row = n_seq - ROW
    n_flow = n_seq // ROW - 1
    tok = q_ref.shape[0]
    kv = k_ref.shape[1] // HEAD_WIDTH
    half = tok // 2
    span = 2 * tok + half
    has_prev = me >= 2
    has_pair = me >= 1
    has_next = me < n_seq - 2
    turns = jnp.logical_and(place >= ROW - 2, has_next)
    lands = jnp.logical_and(place < 2, has_prev)
    relays = jnp.logical_not(has_next)

    def tp_at(step):
        return lax.rem(tp + n_tp + step, n_tp)

    @pl.when(jnp.logical_not(has_prev))
    def _():
        for buffer in (kall, vraw):
            buffer[:, : 2 * tok, :] = jnp.zeros((kv, 2 * tok, HEAD_WIDTH), buffer.dtype)
        latall[...] = jnp.zeros_like(latall)

    barrier = pltpu.get_barrier_semaphore()

    def greet(device):
        pl.semaphore_signal(barrier, inc=1, device_id=device, device_id_type=MESH)

    greet((partner, tp))

    @pl.when(has_prev)
    def _():
        greet((me - 2, tp))

    @pl.when(jnp.logical_and(has_prev, core == 0))
    def _():
        greet((me - 1, tp))

    for step in range(1, n_tp):
        greet((me, tp_at(step)))

    if DETOUR:
        @pl.when(lands)
        def _():
            greet((n_seq - 2 + core, tp))

        @pl.when(relays)
        def _():
            for flow in range(n_flow):
                greet((flow * ROW + place, tp))

    loads = [
        pltpu.make_async_copy(x_ref, x_v, in_sem.at[0]),
        pltpu.make_async_copy(down_ref, down_v, in_sem.at[1]),
        pltpu.make_async_copy(up_ref, up_v, in_sem.at[2]),
        pltpu.make_async_copy(q_ref, q_v, in_sem.at[3]),
    ]
    loads[0].start()
    loads[1].start()

    def columns(head):
        return pl.ds(pl.multiple_of(head * HEAD_WIDTH, HEAD_WIDTH), HEAD_WIDTH)

    def own_copy(which, head):
        src = (k_ref, v_ref)[which].at[:, columns(head)]
        dst = (kall, vraw)[which].at[head, pl.ds(2 * tok, tok), :]
        return pltpu.make_async_copy(src, dst, kv_sem.at[which, head])

    def ring_copy(which, head, part):
        rows = pl.ds(part * half, half)
        return pltpu.make_async_remote_copy(
            src_ref=(k_ref, v_ref)[which].at[rows, columns(head)],
            dst_ref=(kall, vraw)[which].at[head, rows, :],
            send_sem=ring_send.at[which, head, part],
            recv_sem=ring_recv.at[which, head, part],
            device_id=(me + 2, tp),
            device_id_type=MESH,
        )

    def give_copy(which, head, part):
        rows = pl.ds(part * half, half)
        return pltpu.make_async_remote_copy(
            src_ref=(k_ref, v_ref)[which].at[rows, columns(head)],
            dst_ref=(kall, vraw)[which].at[head, pl.ds(tok + part * half, half), :],
            send_sem=pair_send.at[which, head, part],
            recv_sem=pair_recv.at[which, head, part],
            device_id=(partner, tp),
            device_id_type=MESH,
        )

    def relay_copy(which, head, part):
        buffer = (kall, vraw)[which]
        return pltpu.make_async_remote_copy(
            src_ref=buffer.at[head, pl.ds(part * half, half), :],
            dst_ref=buffer.at[head, pl.ds(tok + part * half, half), :],
            send_sem=pair_send.at[which, head, part],
            recv_sem=pair_recv.at[which, head, part],
            device_id=(partner, tp),
            device_id_type=MESH,
        )

    def hop_copy(flow, index):
        which, head, part = DETOUR[index]
        return pltpu.make_async_remote_copy(
            src_ref=(k_ref, v_ref)[which].at[pl.ds(part * half, half), columns(head)],
            dst_ref=hold.at[flow, index],
            send_sem=hop_send.at[index],
            recv_sem=hop_recv.at[flow, index],
            device_id=(last_row + place, tp),
            device_id_type=MESH,
        )

    def forward_copy(flow, index):
        which, head, part = DETOUR[index]
        return pltpu.make_async_remote_copy(
            src_ref=hold.at[flow, index],
            dst_ref=(kall, vraw)[which].at[head, pl.ds(part * half, half), :],
            send_sem=fwd_send.at[flow, index],
            recv_sem=ring_recv.at[which, head, part],
            device_id=((flow + 1) * ROW + core, tp),
            device_id_type=MESH,
        )

    def forward(indices):
        @pl.when(relays)
        def _():
            for index in indices:
                for flow in list(range(0, n_flow, 2)) + list(range(1, n_flow, 2)):
                    hop_copy(flow, index).wait_recv()
                    forward_copy(flow, index).start()

    def lat_copy(source, target, lane, device):
        return pltpu.make_async_remote_copy(
            src_ref=latall.at[source],
            dst_ref=latall.at[target],
            send_sem=lat_send.at[lane],
            recv_sem=lat_recv.at[lane],
            device_id=(device, tp),
            device_id_type=MESH,
        )

    lat_ring = functools.partial(lat_copy, 2, 0, 0, me + 2)
    lat_give = functools.partial(lat_copy, 2, 1, 1, partner)
    lat_cross = functools.partial(lat_copy, 2, 1, 1, me + 1)

    expected = n_tp + (1 + core) * has_next.astype(jnp.int32)
    if DETOUR:
        expected = expected + turns.astype(jnp.int32) + n_flow * relays.astype(jnp.int32)
    pl.semaphore_wait(barrier, expected)

    order = [(w, h, p) for h in range(kv - 1) for w in range(2) for p in (1, 0)]
    order += [(w, kv - 1, p) for p in (1, 0) for w in range(2)]

    straight = jnp.logical_and(has_next, jnp.logical_not(turns))

    def send(first, last):
        @pl.when(straight)
        def _():
            for item in order[first:last]:
                ring_copy(*item).start()

        @pl.when(turns)
        def _():
            for item in [item for item in order if item not in DETOUR][first:last]:
                ring_copy(*item).start()

    if DETOUR:
        @pl.when(turns)
        def _():
            for index in range(len(DETOUR)):
                hop_copy(lax.div(me, ROW), index).start()

    send(0, EARLY)

    @pl.when(core == 0)
    def _():
        for item in order:
            give_copy(*item).start()

    loads[0].wait()
    loads[1].wait()
    for load in loads[2:]:
        load.start()
    for head in range(kv):
        own_copy(0, head).start()
        own_copy(1, head).start()
    lat[tp] = jnp.dot(
        down_v[choice_ref[(me * tok) // SEG_LEN]], x_v[...], preferred_element_type=jnp.float32
    )

    def part_copy(step):
        return pltpu.make_async_remote_copy(
            src_ref=lat.at[tp],
            dst_ref=lat.at[tp],
            send_sem=part_send.at[step - 1],
            recv_sem=part_recv.at[step - 1],
            device_id=(me, tp_at(step)),
            device_id_type=MESH,
        )

    def part_arrival(step):
        slot = lat.at[tp_at(-step)]
        return pltpu.make_async_remote_copy(
            src_ref=slot,
            dst_ref=slot,
            send_sem=part_send.at[step - 1],
            recv_sem=part_recv.at[step - 1],
            device_id=(me, tp_at(step)),
            device_id_type=MESH,
        )

    for step in range(1, n_tp):
        part_copy(step).start()

    forward(range(0, min(1, len(DETOUR))))

    loads[2].wait()
    for source in range(3):
        segment = (jnp.maximum(me + source - 2, 0) * tok) // SEG_LEN
        upsel[source] = up_v[choice_ref[segment]]

    for step in range(1, n_tp):
        part_arrival(step).wait_recv()
    total = lat[0]
    for step in range(1, n_tp):
        total = total + lat[step]
    latall[2] = total.astype(jnp.bfloat16)

    @pl.when(core == 0)
    def _():
        lat_give().start()

    @pl.when(has_next)
    def _():
        @pl.when(core == 1)
        def _():
            lat_cross().start()

        lat_ring().start()

    send(EARLY, None)

    forward(range(1, len(DETOUR)))

    loads[3].wait()

    @pl.when(has_prev)
    def _():
        lat_ring().wait_recv()

    @pl.when(has_pair)
    def _():
        lat_give().wait_recv()

    row = lax.broadcasted_iota(jnp.int32, (half, half), 0)
    col = lax.broadcasted_iota(jnp.int32, (half, half), 1)
    later = col > row
    have = [has_prev, has_pair, None]

    def arrive(head, part):
        @pl.when(has_prev)
        def _():
            for which in range(2):
                ring_copy(which, head, part).wait_recv()

                @pl.when(core == 1)
                def _():
                    relay_copy(which, head, part).start()

    def arrive_pair(head, part):
        @pl.when(has_pair)
        def _():
            for which in range(2):
                give_copy(which, head, part).wait_recv()

    def fill_values(head, source, part, count):
        update = lax.dot_general(
            latall[source, :, pl.ds(part * half, count * half)], upsel[source, :, columns(head)],
            (((0,), (0,)), ((), ())), preferred_element_type=jnp.float32,
        )
        rows = pl.ds(source * tok + part * half, count * half)
        vf[rows, :] = (vraw[head, rows, :].astype(jnp.float32) + update).astype(jnp.bfloat16)

    def attend(head, block, member, runs, keep=False, resume=False):
        at = columns(2 * head + member)
        rows = q_v[pl.ds(block * half, half), at]
        scores, tops = [], {}
        for start, segments in runs:
            width = sum(segment[0] for segment in segments)
            s = lax.dot_general(
                rows, kall[head, pl.ds(start, width), :],
                (((1,), (1,)), ((), ())), preferred_element_type=jnp.float32,
            )
            cut = []
            first = 0
            for length, source, mask in segments:
                piece = s[:, first : first + length]
                if mask == "far":
                    piece = jnp.where(later, piece, NEG)
                if mask == "own":
                    piece = jnp.where(later, NEG, piece)
                cut.append(piece)
                tops.setdefault(source, []).append(piece)
                first += length
            scores.append(cut)
        top = None
        for source, pieces in tops.items():
            part = jnp.max(
                pieces[0] if len(pieces) == 1 else jnp.concatenate(pieces, axis=1),
                axis=1, keepdims=True,
            )
            if have[source] is not None:
                part = jnp.where(have[source], part, NEG)
            top = part if top is None else jnp.maximum(top, part)
        top = top * SCALE2
        if resume:
            old = m_s[block, member]
            top = jnp.maximum(top, old)
            fade = jnp.exp2(old - top)
        shift = {
            source: top if have[source] is None else jnp.where(have[source], top, BIG)
            for source in tops
        }
        norm, out = None, None
        for cut, (start, segments) in zip(scores, runs):
            expo = [
                jnp.exp2(piece * SCALE2 - shift[source])
                for piece, (_, source, _) in zip(cut, segments)
            ]
            expo = expo[0] if len(expo) == 1 else jnp.concatenate(expo, axis=1)
            part = jnp.sum(expo, axis=1, keepdims=True)
            norm = part if norm is None else norm + part
            part = jnp.dot(
                expo.astype(jnp.bfloat16), vf[pl.ds(start, expo.shape[1]), :],
                preferred_element_type=jnp.float32,
            )
            out = part if out is None else out + part
        if resume:
            norm = norm + fade * l_s[block, member]
            out = out + fade * acc_s[block, member]
        if keep:
            m_s[block, member] = top
            l_s[block, member] = norm
            acc_s[block, member] = out
        else:
            out_ref[pl.ds(block * half, half), at] = (out / norm).astype(jnp.bfloat16)

    def one_head(head, carry):
        own_copy(0, head).wait()
        own_copy(1, head).wait()
        for part in (1, 0):
            arrive(head, part)
        for part in (1, 0):
            arrive_pair(head, part)
        for source in range(3):
            fill_values(head, source, 0, 2)
        for member in range(2):
            attend(head, 0, member, [
                (0, [(half, 0, "far"), (half, 0, None), (tok, 1, None), (half, 2, "own")]),
            ])
            attend(head, 1, member, [
                (half, [(half, 0, "far"), (tok, 1, None), (half, 2, None), (half, 2, "own")]),
            ])
        return carry

    lax.fori_loop(0, kv - 1, one_head, 0)

    head = kv - 1
    own_copy(0, head).wait()
    own_copy(1, head).wait()
    fill_values(head, 2, 0, 2)
    arrive(head, 1)
    fill_values(head, 0, 1, 1)
    arrive_pair(head, 1)
    fill_values(head, 1, 1, 1)
    for member in range(2):
        attend(head, 0, member, [
            (half, [(half, 0, None)]),
            (tok + half, [(half, 1, None), (half, 2, "own")]),
        ], keep=True)
        attend(head, 1, member, [
            (half, [(half, 0, "far")]),
            (tok + half, [(half, 1, None), (half, 2, None), (half, 2, "own")]),
        ], keep=True)
    arrive(head, 0)
    fill_values(head, 0, 0, 1)
    arrive_pair(head, 0)
    fill_values(head, 1, 0, 1)
    for member in range(2):
        attend(head, 0, member, [
            (0, [(half, 0, "far")]),
            (tok, [(half, 1, None)]),
        ], resume=True)
        attend(head, 1, member, [
            (tok, [(half, 1, None)]),
        ], resume=True)

    for step in range(1, n_tp):
        part_copy(step).wait_send()

    @pl.when(has_next)
    def _():
        lat_ring().wait_send()
        for item in order:
            if item not in DETOUR:
                ring_copy(*item).wait_send()

    if DETOUR:
        @pl.when(straight)
        def _():
            for item in DETOUR:
                ring_copy(*item).wait_send()

        @pl.when(turns)
        def _():
            for index in range(len(DETOUR)):
                hop_copy(lax.div(me, ROW), index).wait_send()

        @pl.when(relays)
        def _():
            for index in range(len(DETOUR)):
                for flow in range(n_flow):
                    forward_copy(flow, index).wait_send()

    @pl.when(jnp.logical_or(core == 0, has_next))
    def _():
        lat_give().wait_send()

    @pl.when(jnp.logical_or(core == 0, has_prev))
    def _():
        for item in order:
            give_copy(*item).wait_send()


def on_device(
    n_seq, n_tp,
    normed_input, query, key, value, adapter_down_maps, adapter_up_maps, block_adapter_choice,
):
    tok, width = normed_input.shape
    kv = key.shape[1] // HEAD_WIDTH
    count, rank, columns = adapter_up_maps.shape
    n_flow = n_seq // ROW - 1
    n_hop = max(1, len(DETOUR))
    bf16, f32 = jnp.bfloat16, jnp.float32
    dma = pltpu.SemaphoreType.DMA
    hbm = pl.BlockSpec(memory_space=pl.ANY)
    return pl.pallas_call(
        functools.partial(kernel, n_seq, n_tp),
        out_shape=pltpu.VMEM(query.shape, bf16),
        in_specs=[pl.BlockSpec(memory_space=pltpu.SMEM)] + [hbm] * 6,
        out_specs=pl.BlockSpec(memory_space=pltpu.VMEM),
        scratch_shapes=[
            pltpu.VMEM((width, tok), bf16),
            pltpu.VMEM((count, rank, width), bf16),
            pltpu.VMEM((count, rank, columns), bf16),
            pltpu.VMEM(query.shape, bf16),
            pltpu.VMEM((kv, 3 * tok, HEAD_WIDTH), bf16),
            pltpu.VMEM((kv, 3 * tok, HEAD_WIDTH), bf16),
            pltpu.VMEM((3 * tok, HEAD_WIDTH), bf16),
            pltpu.VMEM((n_tp, rank, tok), f32),
            pltpu.VMEM((3, rank, tok), bf16),
            pltpu.VMEM((3, rank, columns), bf16),
            pltpu.VMEM((n_flow, n_hop, tok // 2, HEAD_WIDTH), bf16),
            pltpu.VMEM((2, 2, tok // 2, 1), f32),
            pltpu.VMEM((2, 2, tok // 2, 1), f32),
            pltpu.VMEM((2, 2, tok // 2, HEAD_WIDTH), f32),
            dma((4,)),
            dma((2, kv)),
            dma((2, kv, 2)), dma((2, kv, 2)), dma((2, kv, 2)), dma((2, kv, 2)),
            dma((n_tp - 1,)), dma((n_tp - 1,)), dma((2,)), dma((2,)),
            dma((n_hop,)), dma((n_flow, n_hop)), dma((n_flow, n_hop)),
        ],
        compiler_params=pltpu.CompilerParams(collective_id=0, has_side_effects=True),
    )(
        block_adapter_choice, normed_input.T, query, key, value,
        adapter_down_maps, adapter_up_maps,
    )


def solution(mesh):
    placed = (
        P("seq", "tp"),
        P("seq", "tp"),
        P("seq", "tp"),
        P("seq", "tp"),
        P(None, None, "tp"),
        P(None, None, "tp"),
        P(),
    )
    return jax.shard_map(
        functools.partial(on_device, mesh.shape["seq"], mesh.shape["tp"]),
        mesh=mesh, in_specs=placed, out_specs=P("seq", "tp"), check_vma=False,
    )
```

```python
import functools

import jax
import jax.numpy as jnp
from jax import lax
from jax.experimental import pallas as pl
from jax.experimental.pallas import tpu as pltpu
from jax.sharding import PartitionSpec as P

HEAD_WIDTH = 128
SEG_LEN = 2048
MESH = pl.DeviceIdType.MESH
EARLY = 6
QUERY_SCALE = 168.0 ** (-0.5)
NEG = -1e30
BIG = 1e30
ROW = 16
DETOUR = ((1, 1, 0), (1, 2, 0), (1, 3, 0))


def kernel(
    n_seq, n_tp,
    choice_ref, x_ref, q_ref, k_ref, v_ref, down_ref, up_ref,
    out_ref,
    x_v, down_v, up_v, q_v, kall, vraw, vf, lat, latall, upsel, hold, m_s, acc_s,
    in_sem, kv_sem,
    ring_send, ring_recv, pair_send, pair_recv,
    part_send, part_recv, lat_send, lat_recv,
    hop_send, hop_recv, fwd_send,
):
    me = lax.axis_index("seq")
    tp = lax.axis_index("tp")
    core = lax.rem(me, 2)
    partner = me + 1 - 2 * core
    place = lax.rem(me, ROW)
    last_row = n_seq - ROW
    n_flow = n_seq // ROW - 1
    tok = q_ref.shape[0]
    kv = k_ref.shape[1] // HEAD_WIDTH
    half = tok // 2
    span = 2 * tok + half
    has_prev = me >= 2
    has_pair = me >= 1
    has_next = me < n_seq - 2
    turns = jnp.logical_and(place >= ROW - 2, has_next)
    lands = jnp.logical_and(place < 2, has_prev)
    relays = jnp.logical_not(has_next)

    def tp_at(step):
        return lax.rem(tp + n_tp + step, n_tp)

    @pl.when(jnp.logical_not(has_prev))
    def _():
        for buffer in (kall, vraw):
            buffer[:, : 2 * tok, :] = jnp.zeros((kv, 2 * tok, HEAD_WIDTH), buffer.dtype)
        latall[...] = jnp.zeros_like(latall)

    barrier = pltpu.get_barrier_semaphore()

    def greet(device):
        pl.semaphore_signal(barrier, inc=1, device_id=device, device_id_type=MESH)

    greet((partner, tp))

    @pl.when(has_prev)
    def _():
        greet((me - 2, tp))

    @pl.when(jnp.logical_and(has_prev, core == 0))
    def _():
        greet((me - 1, tp))

    for step in range(1, n_tp):
        greet((me, tp_at(step)))

    if DETOUR:
        @pl.when(lands)
        def _():
            greet((n_seq - 2 + core, tp))

        @pl.when(relays)
        def _():
            for flow in range(n_flow):
                greet((flow * ROW + place, tp))

    loads = [
        pltpu.make_async_copy(x_ref, x_v, in_sem.at[0]),
        pltpu.make_async_copy(down_ref, down_v, in_sem.at[1]),
        pltpu.make_async_copy(up_ref, up_v, in_sem.at[2]),
        pltpu.make_async_copy(q_ref, q_v, in_sem.at[3]),
    ]
    loads[0].start()
    loads[1].start()

    def columns(head):
        return pl.ds(pl.multiple_of(head * HEAD_WIDTH, HEAD_WIDTH), HEAD_WIDTH)

    def own_copy(which, head):
        src = (k_ref, v_ref)[which].at[:, columns(head)]
        dst = (kall, vraw)[which].at[head, pl.ds(2 * tok, tok), :]
        return pltpu.make_async_copy(src, dst, kv_sem.at[which, head])

    def ring_copy(which, head, part):
        rows = pl.ds(part * half, half)
        return pltpu.make_async_remote_copy(
            src_ref=(k_ref, v_ref)[which].at[rows, columns(head)],
            dst_ref=(kall, vraw)[which].at[head, rows, :],
            send_sem=ring_send.at[which, head, part],
            recv_sem=ring_recv.at[which, head, part],
            device_id=(me + 2, tp),
            device_id_type=MESH,
        )

    def give_copy(which, head, part):
        rows = pl.ds(part * half, half)
        return pltpu.make_async_remote_copy(
            src_ref=(k_ref, v_ref)[which].at[rows, columns(head)],
            dst_ref=(kall, vraw)[which].at[head, pl.ds(tok + part * half, half), :],
            send_sem=pair_send.at[which, head, part],
            recv_sem=pair_recv.at[which, head, part],
            device_id=(partner, tp),
            device_id_type=MESH,
        )

    def relay_copy(which, head, part):
        buffer = (kall, vraw)[which]
        return pltpu.make_async_remote_copy(
            src_ref=buffer.at[head, pl.ds(part * half, half), :],
            dst_ref=buffer.at[head, pl.ds(tok + part * half, half), :],
            send_sem=pair_send.at[which, head, part],
            recv_sem=pair_recv.at[which, head, part],
            device_id=(partner, tp),
            device_id_type=MESH,
        )

    def hop_copy(flow, index):
        which, head, part = DETOUR[index]
        return pltpu.make_async_remote_copy(
            src_ref=(k_ref, v_ref)[which].at[pl.ds(part * half, half), columns(head)],
            dst_ref=hold.at[flow, index],
            send_sem=hop_send.at[index],
            recv_sem=hop_recv.at[flow, index],
            device_id=(last_row + place, tp),
            device_id_type=MESH,
        )

    def forward_copy(flow, index):
        which, head, part = DETOUR[index]
        return pltpu.make_async_remote_copy(
            src_ref=hold.at[flow, index],
            dst_ref=(kall, vraw)[which].at[head, pl.ds(part * half, half), :],
            send_sem=fwd_send.at[flow, index],
            recv_sem=ring_recv.at[which, head, part],
            device_id=((flow + 1) * ROW + core, tp),
            device_id_type=MESH,
        )

    def forward(indices):
        @pl.when(relays)
        def _():
            for index in indices:
                for flow in (1, 0, 2):
                    hop_copy(flow, index).wait_recv()
                    forward_copy(flow, index).start()

    def lat_copy(source, target, lane, device):
        return pltpu.make_async_remote_copy(
            src_ref=latall.at[source],
            dst_ref=latall.at[target],
            send_sem=lat_send.at[lane],
            recv_sem=lat_recv.at[lane],
            device_id=(device, tp),
            device_id_type=MESH,
        )

    lat_ring = functools.partial(lat_copy, 2, 0, 0, me + 2)
    lat_give = functools.partial(lat_copy, 2, 1, 1, partner)
    lat_cross = functools.partial(lat_copy, 2, 1, 1, me + 1)

    expected = n_tp + (1 + core) * has_next.astype(jnp.int32)
    if DETOUR:
        expected = expected + turns.astype(jnp.int32) + n_flow * relays.astype(jnp.int32)
    pl.semaphore_wait(barrier, expected)

    order = [(w, h, p) for h in range(kv - 1) for w in range(2) for p in (1, 0)]
    order += [(w, kv - 1, p) for p in (1, 0) for w in range(2)]

    straight = jnp.logical_and(has_next, jnp.logical_not(turns))

    def send(first, last):
        @pl.when(straight)
        def _():
            for item in order[first:last]:
                ring_copy(*item).start()

        @pl.when(turns)
        def _():
            for item in [item for item in order if item not in DETOUR][first:last]:
                ring_copy(*item).start()

    if DETOUR:
        @pl.when(turns)
        def _():
            for index in range(len(DETOUR)):
                hop_copy(lax.div(me, ROW), index).start()

    send(0, EARLY)

    @pl.when(core == 0)
    def _():
        for item in order:
            give_copy(*item).start()

    vf[:, HEAD_WIDTH:] = jnp.ones((3 * tok, HEAD_WIDTH), vf.dtype)

    loads[0].wait()
    loads[1].wait()
    for load in loads[2:]:
        load.start()
    for head in range(kv):
        own_copy(0, head).start()
        own_copy(1, head).start()
    lat[tp] = jnp.dot(
        down_v[choice_ref[(me * tok) // SEG_LEN]], x_v[...], preferred_element_type=jnp.float32
    )

    def part_copy(step):
        return pltpu.make_async_remote_copy(
            src_ref=lat.at[tp],
            dst_ref=lat.at[tp],
            send_sem=part_send.at[step - 1],
            recv_sem=part_recv.at[step - 1],
            device_id=(me, tp_at(step)),
            device_id_type=MESH,
        )

    def part_arrival(step):
        slot = lat.at[tp_at(-step)]
        return pltpu.make_async_remote_copy(
            src_ref=slot,
            dst_ref=slot,
            send_sem=part_send.at[step - 1],
            recv_sem=part_recv.at[step - 1],
            device_id=(me, tp_at(step)),
            device_id_type=MESH,
        )

    for step in range(1, n_tp):
        part_copy(step).start()

    forward(range(len(DETOUR)))

    loads[2].wait()
    for source in range(3):
        segment = (jnp.maximum(me + source - 2, 0) * tok) // SEG_LEN
        upsel[source] = up_v[choice_ref[segment]]

    for step in range(1, n_tp):
        part_arrival(step).wait_recv()
    total = lat[0]
    for step in range(1, n_tp):
        total = total + lat[step]
    latall[2] = total.astype(jnp.bfloat16)

    @pl.when(core == 0)
    def _():
        lat_give().start()

    @pl.when(has_next)
    def _():
        @pl.when(core == 1)
        def _():
            lat_cross().start()

        lat_ring().start()

    send(EARLY, None)

    loads[3].wait()

    @pl.when(has_prev)
    def _():
        lat_ring().wait_recv()

    @pl.when(has_pair)
    def _():
        lat_give().wait_recv()

    row = lax.broadcasted_iota(jnp.int32, (half, half), 0)
    col = lax.broadcasted_iota(jnp.int32, (half, half), 1)
    later = col > row
    have = [has_prev, has_pair, None]

    def arrive(head, part):
        @pl.when(has_prev)
        def _():
            for which in range(2):
                ring_copy(which, head, part).wait_recv()

                @pl.when(core == 1)
                def _():
                    relay_copy(which, head, part).start()

    def arrive_pair(head, part):
        @pl.when(has_pair)
        def _():
            for which in range(2):
                give_copy(which, head, part).wait_recv()

    def fill_values(head, source, part, count):
        update = lax.dot_general(
            latall[source, :, pl.ds(part * half, count * half)], upsel[source, :, columns(head)],
            (((0,), (0,)), ((), ())), preferred_element_type=jnp.float32,
        )
        rows = pl.ds(source * tok + part * half, count * half)
        vf[rows, :HEAD_WIDTH] = (vraw[head, rows, :].astype(jnp.float32) + update).astype(jnp.bfloat16)

    def attend(head, jobs, keep=False, resume=False):
        scores = []
        for block, member, runs in jobs:
            rows = q_v[pl.ds(block * half, half), columns(2 * head + member)]
            parts = []
            for start, segments in runs:
                width = sum(segment[0] for segment in segments)
                s = lax.dot_general(
                    rows, kall[head, pl.ds(start, width), :],
                    (((1,), (1,)), ((), ())), preferred_element_type=jnp.float32,
                )
                cut = []
                first = 0
                for length, _, mask in segments:
                    piece = s[:, first : first + length]
                    if mask == "far":
                        piece = jnp.where(later, piece, NEG)
                    if mask == "own":
                        piece = jnp.where(later, NEG, piece)
                    cut.append(piece)
                    first += length
                parts.append(cut)
            scores.append(parts)
        tops, fades = [], []
        for (block, member, runs), parts in zip(jobs, scores):
            found = {}
            for cut, (_, segments) in zip(parts, runs):
                for piece, (_, source, _) in zip(cut, segments):
                    found.setdefault(source, []).append(piece)
            top = None
            for source, pieces in found.items():
                part = jnp.max(
                    pieces[0] if len(pieces) == 1 else jnp.concatenate(pieces, axis=1),
                    axis=1, keepdims=True,
                )
                if have[source] is not None:
                    part = jnp.where(have[source], part, NEG)
                top = part if top is None else jnp.maximum(top, part)
            top = top * QUERY_SCALE
            if resume:
                old = m_s[block, member]
                top = jnp.maximum(top, old)
                fades.append(jnp.exp(old - top))
            tops.append(top)
        weights = []
        for (block, member, runs), parts, top in zip(jobs, scores, tops):
            shift = [jnp.where(known, top, BIG) if known is not None else top for known in have]
            weights.append([
                [
                    jnp.exp(piece * QUERY_SCALE - shift[source]).astype(jnp.bfloat16)
                    for piece, (_, source, _) in zip(cut, segments)
                ]
                for cut, (_, segments) in zip(parts, runs)
            ])
        for index, (block, member, runs) in enumerate(jobs):
            out = None
            for cut, (start, _) in zip(weights[index], runs):
                expo = cut[0] if len(cut) == 1 else jnp.concatenate(cut, axis=1)
                part = jnp.dot(
                    expo, vf[pl.ds(start, expo.shape[1]), :], preferred_element_type=jnp.float32
                )
                out = part if out is None else out + part
            if resume:
                out = out + fades[index] * acc_s[block, member]
            if keep:
                m_s[block, member] = tops[index]
                acc_s[block, member] = out
            else:
                out = out[:, :HEAD_WIDTH] / out[:, HEAD_WIDTH:]
                out_ref[pl.ds(block * half, half), columns(2 * head + member)] = out.astype(
                    jnp.bfloat16
                )

    def one_head(head, carry):
        own_copy(0, head).wait()
        own_copy(1, head).wait()
        for part in (1, 0):
            arrive(head, part)
        for part in (1, 0):
            arrive_pair(head, part)
        for source in range(3):
            fill_values(head, source, 0, 2)
        near = [(0, [(half, 0, "far"), (half, 0, None), (tok, 1, None), (half, 2, "own")])]
        wide = [(half, [(half, 0, "far"), (tok, 1, None), (half, 2, None), (half, 2, "own")])]
        attend(head, [(0, member, near) for member in range(2)])
        attend(head, [(1, member, wide) for member in range(2)])
        return carry

    lax.fori_loop(0, kv - 1, one_head, 0)

    head = kv - 1
    own_copy(0, head).wait()
    own_copy(1, head).wait()
    fill_values(head, 2, 0, 2)
    arrive(head, 1)
    fill_values(head, 0, 1, 1)
    arrive_pair(head, 1)
    fill_values(head, 1, 1, 1)
    near = [(half, [(half, 0, None)]), (tok + half, [(half, 1, None), (half, 2, "own")])]
    wide = [
        (half, [(half, 0, "far")]),
        (tok + half, [(half, 1, None), (half, 2, None), (half, 2, "own")]),
    ]
    attend(head, [(0, member, near) for member in range(2)], keep=True)
    attend(head, [(1, member, wide) for member in range(2)], keep=True)
    arrive(head, 0)
    fill_values(head, 0, 0, 1)
    arrive_pair(head, 0)
    fill_values(head, 1, 0, 1)
    near = [(0, [(half, 0, "far")]), (tok, [(half, 1, None)])]
    wide = [(tok, [(half, 1, None)])]
    attend(
        head,
        [(0, member, near) for member in range(2)] + [(1, member, wide) for member in range(2)],
        resume=True,
    )

    for step in range(1, n_tp):
        part_copy(step).wait_send()

    @pl.when(has_next)
    def _():
        lat_ring().wait_send()
        for item in order:
            if item not in DETOUR:
                ring_copy(*item).wait_send()

    if DETOUR:
        @pl.when(straight)
        def _():
            for item in DETOUR:
                ring_copy(*item).wait_send()

        @pl.when(turns)
        def _():
            for index in range(len(DETOUR)):
                hop_copy(lax.div(me, ROW), index).wait_send()

        @pl.when(relays)
        def _():
            for index in range(len(DETOUR)):
                for flow in range(n_flow):
                    forward_copy(flow, index).wait_send()

    @pl.when(jnp.logical_or(core == 0, has_next))
    def _():
        lat_give().wait_send()

    @pl.when(jnp.logical_or(core == 0, has_prev))
    def _():
        for item in order:
            give_copy(*item).wait_send()


def on_device(
    n_seq, n_tp,
    normed_input, query, key, value, adapter_down_maps, adapter_up_maps, block_adapter_choice,
):
    tok, width = normed_input.shape
    kv = key.shape[1] // HEAD_WIDTH
    count, rank, columns = adapter_up_maps.shape
    n_flow = n_seq // ROW - 1
    n_hop = max(1, len(DETOUR))
    bf16, f32 = jnp.bfloat16, jnp.float32
    dma = pltpu.SemaphoreType.DMA
    hbm = pl.BlockSpec(memory_space=pl.ANY)
    return pl.pallas_call(
        functools.partial(kernel, n_seq, n_tp),
        out_shape=pltpu.VMEM(query.shape, bf16),
        in_specs=[pl.BlockSpec(memory_space=pltpu.SMEM)] + [hbm] * 6,
        out_specs=pl.BlockSpec(memory_space=pltpu.VMEM),
        scratch_shapes=[
            pltpu.VMEM((width, tok), bf16),
            pltpu.VMEM((count, rank, width), bf16),
            pltpu.VMEM((count, rank, columns), bf16),
            pltpu.VMEM(query.shape, bf16),
            pltpu.VMEM((kv, 3 * tok, HEAD_WIDTH), bf16),
            pltpu.VMEM((kv, 3 * tok, HEAD_WIDTH), bf16),
            pltpu.VMEM((3 * tok, 2 * HEAD_WIDTH), bf16),
            pltpu.VMEM((n_tp, rank, tok), f32),
            pltpu.VMEM((3, rank, tok), bf16),
            pltpu.VMEM((3, rank, columns), bf16),
            pltpu.VMEM((n_flow, n_hop, tok // 2, HEAD_WIDTH), bf16),
            pltpu.VMEM((2, 2, tok // 2, 1), f32),
            pltpu.VMEM((2, 2, tok // 2, 2 * HEAD_WIDTH), f32),
            dma((4,)),
            dma((2, kv)),
            dma((2, kv, 2)), dma((2, kv, 2)), dma((2, kv, 2)), dma((2, kv, 2)),
            dma((n_tp - 1,)), dma((n_tp - 1,)), dma((2,)), dma((2,)),
            dma((n_hop,)), dma((n_flow, n_hop)), dma((n_flow, n_hop)),
        ],
        compiler_params=pltpu.CompilerParams(collective_id=0, has_side_effects=True),
    )(
        block_adapter_choice, normed_input.T, query, key, value,
        adapter_down_maps, adapter_up_maps,
    )


def solution(mesh):
    placed = (
        P("seq", "tp"),
        P("seq", "tp"),
        P("seq", "tp"),
        P("seq", "tp"),
        P(None, None, "tp"),
        P(None, None, "tp"),
        P(),
    )
    return jax.shard_map(
        functools.partial(on_device, mesh.shape["seq"], mesh.shape["tp"]),
        mesh=mesh, in_specs=placed, out_specs=P("seq", "tp"), check_vma=False,
    )
```

```python
import functools

import jax
import jax.numpy as jnp
from jax import lax
from jax.experimental import pallas as pl
from jax.experimental.pallas import tpu as pltpu
from jax.sharding import PartitionSpec as P

HEAD_WIDTH = 128
SEG_LEN = 2048
MESH = pl.DeviceIdType.MESH
EARLY = 6
QUERY_SCALE = 168.0 ** (-0.5)
NEG = -1e30
BIG = 1e30
ROW = 16
DETOUR = ((1, 1, 0), (1, 2, 0), (1, 3, 0))


def kernel(
    n_seq, n_tp,
    choice_ref, x_ref, q_ref, k_ref, v_ref, down_ref, up_ref,
    out_ref,
    x_v, down_v, up_v, q_v, kall, vraw, vf, lat, latall, upsel, hold, m_s, acc_s,
    in_sem, kv_sem,
    ring_send, ring_recv, pair_send, pair_recv,
    part_send, part_recv, lat_send, lat_recv,
    hop_send, hop_recv, fwd_send,
):
    me = lax.axis_index("seq")
    tp = lax.axis_index("tp")
    core = lax.rem(me, 2)
    partner = me + 1 - 2 * core
    place = lax.rem(me, ROW)
    last_row = n_seq - ROW
    n_flow = n_seq // ROW - 1
    tok = q_ref.shape[0]
    kv = k_ref.shape[1] // HEAD_WIDTH
    half = tok // 2
    span = 2 * tok + half
    has_prev = me >= 2
    has_pair = me >= 1
    has_next = me < n_seq - 2
    turns = jnp.logical_and(place >= ROW - 2, has_next)
    lands = jnp.logical_and(place < 2, has_prev)
    relays = jnp.logical_not(has_next)

    def tp_at(step):
        return lax.rem(tp + n_tp + step, n_tp)

    @pl.when(jnp.logical_not(has_prev))
    def _():
        for buffer in (kall, vraw):
            buffer[:, : 2 * tok, :] = jnp.zeros((kv, 2 * tok, HEAD_WIDTH), buffer.dtype)
        latall[...] = jnp.zeros_like(latall)

    barrier = pltpu.get_barrier_semaphore()

    def greet(device):
        pl.semaphore_signal(barrier, inc=1, device_id=device, device_id_type=MESH)

    greet((partner, tp))

    @pl.when(has_prev)
    def _():
        greet((me - 2, tp))

    @pl.when(jnp.logical_and(has_prev, core == 0))
    def _():
        greet((me - 1, tp))

    for step in range(1, n_tp):
        greet((me, tp_at(step)))

    if DETOUR:
        @pl.when(lands)
        def _():
            greet((n_seq - 2 + core, tp))

        @pl.when(relays)
        def _():
            for flow in range(n_flow):
                greet((flow * ROW + place, tp))

    loads = [
        pltpu.make_async_copy(x_ref, x_v, in_sem.at[0]),
        pltpu.make_async_copy(down_ref, down_v, in_sem.at[1]),
        pltpu.make_async_copy(up_ref, up_v, in_sem.at[2]),
        pltpu.make_async_copy(q_ref, q_v, in_sem.at[3]),
    ]
    loads[0].start()
    loads[1].start()

    def columns(head):
        return pl.ds(pl.multiple_of(head * HEAD_WIDTH, HEAD_WIDTH), HEAD_WIDTH)

    def own_copy(which, head):
        src = (k_ref, v_ref)[which].at[:, columns(head)]
        dst = (kall, vraw)[which].at[head, pl.ds(2 * tok, tok), :]
        return pltpu.make_async_copy(src, dst, kv_sem.at[which, head])

    def ring_copy(which, head, part):
        rows = pl.ds(part * half, half)
        return pltpu.make_async_remote_copy(
            src_ref=(k_ref, v_ref)[which].at[rows, columns(head)],
            dst_ref=(kall, vraw)[which].at[head, rows, :],
            send_sem=ring_send.at[which, head, part],
            recv_sem=ring_recv.at[which, head, part],
            device_id=(me + 2, tp),
            device_id_type=MESH,
        )

    def give_copy(which, head, part):
        rows = pl.ds(part * half, half)
        return pltpu.make_async_remote_copy(
            src_ref=(k_ref, v_ref)[which].at[rows, columns(head)],
            dst_ref=(kall, vraw)[which].at[head, pl.ds(tok + part * half, half), :],
            send_sem=pair_send.at[which, head, part],
            recv_sem=pair_recv.at[which, head, part],
            device_id=(partner, tp),
            device_id_type=MESH,
        )

    def relay_copy(which, head, part):
        buffer = (kall, vraw)[which]
        return pltpu.make_async_remote_copy(
            src_ref=buffer.at[head, pl.ds(part * half, half), :],
            dst_ref=buffer.at[head, pl.ds(tok + part * half, half), :],
            send_sem=pair_send.at[which, head, part],
            recv_sem=pair_recv.at[which, head, part],
            device_id=(partner, tp),
            device_id_type=MESH,
        )

    def hop_copy(flow, index):
        which, head, part = DETOUR[index]
        return pltpu.make_async_remote_copy(
            src_ref=(k_ref, v_ref)[which].at[pl.ds(part * half, half), columns(head)],
            dst_ref=hold.at[flow, index],
            send_sem=hop_send.at[index],
            recv_sem=hop_recv.at[flow, index],
            device_id=(last_row + place, tp),
            device_id_type=MESH,
        )

    def forward_copy(flow, index):
        which, head, part = DETOUR[index]
        return pltpu.make_async_remote_copy(
            src_ref=hold.at[flow, index],
            dst_ref=(kall, vraw)[which].at[head, pl.ds(part * half, half), :],
            send_sem=fwd_send.at[flow, index],
            recv_sem=ring_recv.at[which, head, part],
            device_id=((flow + 1) * ROW + core, tp),
            device_id_type=MESH,
        )

    def forward(indices):
        @pl.when(relays)
        def _():
            for index in indices:
                for flow in (1, 0, 2):
                    hop_copy(flow, index).wait_recv()
                    forward_copy(flow, index).start()

    def lat_copy(source, target, lane, device):
        return pltpu.make_async_remote_copy(
            src_ref=latall.at[source],
            dst_ref=latall.at[target],
            send_sem=lat_send.at[lane],
            recv_sem=lat_recv.at[lane],
            device_id=(device, tp),
            device_id_type=MESH,
        )

    lat_ring = functools.partial(lat_copy, 2, 0, 0, me + 2)
    lat_give = functools.partial(lat_copy, 2, 1, 1, partner)
    lat_cross = functools.partial(lat_copy, 2, 1, 1, me + 1)

    expected = n_tp + (1 + core) * has_next.astype(jnp.int32)
    if DETOUR:
        expected = expected + turns.astype(jnp.int32) + n_flow * relays.astype(jnp.int32)
    pl.semaphore_wait(barrier, expected)

    order = [(w, h, p) for h in range(kv - 1) for w in range(2) for p in (1, 0)]
    order += [(w, kv - 1, p) for p in (1, 0) for w in range(2)]

    straight = jnp.logical_and(has_next, jnp.logical_not(turns))

    def send(first, last):
        @pl.when(straight)
        def _():
            for item in order[first:last]:
                ring_copy(*item).start()

        @pl.when(turns)
        def _():
            for item in [item for item in order if item not in DETOUR][first:last]:
                ring_copy(*item).start()

    if DETOUR:
        @pl.when(turns)
        def _():
            for index in range(len(DETOUR)):
                hop_copy(lax.div(me, ROW), index).start()

    send(0, EARLY)

    @pl.when(core == 0)
    def _():
        for item in order:
            give_copy(*item).start()

    vf[:, HEAD_WIDTH:] = jnp.ones((3 * tok, HEAD_WIDTH), vf.dtype)

    loads[0].wait()
    loads[1].wait()
    for load in loads[2:]:
        load.start()
    for head in range(kv):
        own_copy(0, head).start()
        own_copy(1, head).start()
    lat[tp] = jnp.dot(
        down_v[choice_ref[(me * tok) // SEG_LEN]], x_v[...], preferred_element_type=jnp.float32
    )

    def part_copy(step):
        return pltpu.make_async_remote_copy(
            src_ref=lat.at[tp],
            dst_ref=lat.at[tp],
            send_sem=part_send.at[step - 1],
            recv_sem=part_recv.at[step - 1],
            device_id=(me, tp_at(step)),
            device_id_type=MESH,
        )

    def part_arrival(step):
        slot = lat.at[tp_at(-step)]
        return pltpu.make_async_remote_copy(
            src_ref=slot,
            dst_ref=slot,
            send_sem=part_send.at[step - 1],
            recv_sem=part_recv.at[step - 1],
            device_id=(me, tp_at(step)),
            device_id_type=MESH,
        )

    for step in range(1, n_tp):
        part_copy(step).start()

    forward(range(len(DETOUR)))

    loads[2].wait()
    for source in range(3):
        segment = (jnp.maximum(me + source - 2, 0) * tok) // SEG_LEN
        upsel[source] = up_v[choice_ref[segment]]

    for step in range(1, n_tp):
        part_arrival(step).wait_recv()
    total = lat[0]
    for step in range(1, n_tp):
        total = total + lat[step]
    latall[2] = total.astype(jnp.bfloat16)

    @pl.when(core == 0)
    def _():
        lat_give().start()

    @pl.when(has_next)
    def _():
        @pl.when(core == 1)
        def _():
            lat_cross().start()

        lat_ring().start()

    send(EARLY, None)

    loads[3].wait()

    @pl.when(has_prev)
    def _():
        lat_ring().wait_recv()

    @pl.when(has_pair)
    def _():
        lat_give().wait_recv()

    row = lax.broadcasted_iota(jnp.int32, (half, half), 0)
    col = lax.broadcasted_iota(jnp.int32, (half, half), 1)
    later = col > row
    have = [has_prev, has_pair, None]

    def arrive(head, part):
        @pl.when(has_prev)
        def _():
            for which in range(2):
                ring_copy(which, head, part).wait_recv()

                @pl.when(core == 1)
                def _():
                    relay_copy(which, head, part).start()

    def arrive_pair(head, part):
        @pl.when(has_pair)
        def _():
            for which in range(2):
                give_copy(which, head, part).wait_recv()

    def update_of(head, source, part, count):
        return lax.dot_general(
            latall[source, :, pl.ds(part * half, count * half)], upsel[source, :, columns(head)],
            (((0,), (0,)), ((), ())), preferred_element_type=jnp.float32,
        )

    def fill_values(head, source, part, count, update=None):
        if update is None:
            update = update_of(head, source, part, count)
        rows = pl.ds(source * tok + part * half, count * half)
        vf[rows, :HEAD_WIDTH] = (vraw[head, rows, :].astype(jnp.float32) + update).astype(jnp.bfloat16)

    def attend(head, jobs, keep=False, resume=False):
        scores = []
        for block, member, runs in jobs:
            rows = q_v[pl.ds(block * half, half), columns(2 * head + member)]
            parts = []
            for start, segments in runs:
                width = sum(segment[0] for segment in segments)
                s = lax.dot_general(
                    rows, kall[head, pl.ds(start, width), :],
                    (((1,), (1,)), ((), ())), preferred_element_type=jnp.float32,
                )
                cut = []
                first = 0
                for length, _, mask in segments:
                    piece = s[:, first : first + length]
                    if mask == "far":
                        piece = jnp.where(later, piece, NEG)
                    if mask == "own":
                        piece = jnp.where(later, NEG, piece)
                    cut.append(piece)
                    first += length
                parts.append(cut)
            scores.append(parts)
        tops, fades = [], []
        for (block, member, runs), parts in zip(jobs, scores):
            found = {}
            for cut, (_, segments) in zip(parts, runs):
                for piece, (_, source, _) in zip(cut, segments):
                    found.setdefault(source, []).append(piece)
            top = None
            for source, pieces in found.items():
                part = jnp.max(
                    pieces[0] if len(pieces) == 1 else jnp.concatenate(pieces, axis=1),
                    axis=1, keepdims=True,
                )
                if have[source] is not None:
                    part = jnp.where(have[source], part, NEG)
                top = part if top is None else jnp.maximum(top, part)
            top = top * QUERY_SCALE
            if resume:
                old = m_s[block, member]
                top = jnp.maximum(top, old)
                fades.append(jnp.exp(old - top))
            tops.append(top)
        weights = []
        for (block, member, runs), parts, top in zip(jobs, scores, tops):
            shift = [jnp.where(known, top, BIG) if known is not None else top for known in have]
            weights.append([
                [
                    jnp.exp(piece * QUERY_SCALE - shift[source]).astype(jnp.bfloat16)
                    for piece, (_, source, _) in zip(cut, segments)
                ]
                for cut, (_, segments) in zip(parts, runs)
            ])
        for index, (block, member, runs) in enumerate(jobs):
            out = None
            for cut, (start, _) in zip(weights[index], runs):
                expo = cut[0] if len(cut) == 1 else jnp.concatenate(cut, axis=1)
                part = jnp.dot(
                    expo, vf[pl.ds(start, expo.shape[1]), :], preferred_element_type=jnp.float32
                )
                out = part if out is None else out + part
            if resume:
                out = out + fades[index] * acc_s[block, member]
            if keep:
                m_s[block, member] = tops[index]
                acc_s[block, member] = out
            else:
                out = out[:, :HEAD_WIDTH] / out[:, HEAD_WIDTH:]
                out_ref[pl.ds(block * half, half), columns(2 * head + member)] = out.astype(
                    jnp.bfloat16
                )

    def one_head(head, carry):
        own_copy(0, head).wait()
        own_copy(1, head).wait()
        for part in (1, 0):
            arrive(head, part)
        for part in (1, 0):
            arrive_pair(head, part)
        for source in range(3):
            fill_values(head, source, 0, 2)
        near = [(0, [(half, 0, "far"), (half, 0, None), (tok, 1, None), (half, 2, "own")])]
        wide = [(half, [(half, 0, "far"), (tok, 1, None), (half, 2, None), (half, 2, "own")])]
        attend(head, [(0, member, near) for member in range(2)])
        attend(head, [(1, member, wide) for member in range(2)])
        return carry

    lax.fori_loop(0, kv - 1, one_head, 0)

    head = kv - 1
    own_copy(0, head).wait()
    own_copy(1, head).wait()
    fill_values(head, 2, 0, 2)
    updates = {
        (source, part): update_of(head, source, part, 1) for source in range(2) for part in range(2)
    }
    arrive(head, 1)
    fill_values(head, 0, 1, 1, updates[0, 1])
    arrive_pair(head, 1)
    fill_values(head, 1, 1, 1, updates[1, 1])
    near = [(half, [(half, 0, None)]), (tok + half, [(half, 1, None), (half, 2, "own")])]
    wide = [
        (half, [(half, 0, "far")]),
        (tok + half, [(half, 1, None), (half, 2, None), (half, 2, "own")]),
    ]
    attend(head, [(0, member, near) for member in range(2)], keep=True)
    attend(head, [(1, member, wide) for member in range(2)], keep=True)
    arrive(head, 0)
    fill_values(head, 0, 0, 1, updates[0, 0])
    arrive_pair(head, 0)
    fill_values(head, 1, 0, 1, updates[1, 0])
    near = [(0, [(half, 0, "far")]), (tok, [(half, 1, None)])]
    wide = [(tok, [(half, 1, None)])]
    attend(
        head,
        [(0, member, near) for member in range(2)] + [(1, member, wide) for member in range(2)],
        resume=True,
    )

    for step in range(1, n_tp):
        part_copy(step).wait_send()

    @pl.when(has_next)
    def _():
        lat_ring().wait_send()
        for item in order:
            if item not in DETOUR:
                ring_copy(*item).wait_send()

    if DETOUR:
        @pl.when(straight)
        def _():
            for item in DETOUR:
                ring_copy(*item).wait_send()

        @pl.when(turns)
        def _():
            for index in range(len(DETOUR)):
                hop_copy(lax.div(me, ROW), index).wait_send()

        @pl.when(relays)
        def _():
            for index in range(len(DETOUR)):
                for flow in range(n_flow):
                    forward_copy(flow, index).wait_send()

    @pl.when(jnp.logical_or(core == 0, has_next))
    def _():
        lat_give().wait_send()

    @pl.when(jnp.logical_or(core == 0, has_prev))
    def _():
        for item in order:
            give_copy(*item).wait_send()


def on_device(
    n_seq, n_tp,
    normed_input, query, key, value, adapter_down_maps, adapter_up_maps, block_adapter_choice,
):
    tok, width = normed_input.shape
    kv = key.shape[1] // HEAD_WIDTH
    count, rank, columns = adapter_up_maps.shape
    n_flow = n_seq // ROW - 1
    n_hop = max(1, len(DETOUR))
    bf16, f32 = jnp.bfloat16, jnp.float32
    dma = pltpu.SemaphoreType.DMA
    hbm = pl.BlockSpec(memory_space=pl.ANY)
    return pl.pallas_call(
        functools.partial(kernel, n_seq, n_tp),
        out_shape=pltpu.VMEM(query.shape, bf16),
        in_specs=[pl.BlockSpec(memory_space=pltpu.SMEM)] + [hbm] * 6,
        out_specs=pl.BlockSpec(memory_space=pltpu.VMEM),
        scratch_shapes=[
            pltpu.VMEM((width, tok), bf16),
            pltpu.VMEM((count, rank, width), bf16),
            pltpu.VMEM((count, rank, columns), bf16),
            pltpu.VMEM(query.shape, bf16),
            pltpu.VMEM((kv, 3 * tok, HEAD_WIDTH), bf16),
            pltpu.VMEM((kv, 3 * tok, HEAD_WIDTH), bf16),
            pltpu.VMEM((3 * tok, 2 * HEAD_WIDTH), bf16),
            pltpu.VMEM((n_tp, rank, tok), f32),
            pltpu.VMEM((3, rank, tok), bf16),
            pltpu.VMEM((3, rank, columns), bf16),
            pltpu.VMEM((n_flow, n_hop, tok // 2, HEAD_WIDTH), bf16),
            pltpu.VMEM((2, 2, tok // 2, 1), f32),
            pltpu.VMEM((2, 2, tok // 2, 2 * HEAD_WIDTH), f32),
            dma((4,)),
            dma((2, kv)),
            dma((2, kv, 2)), dma((2, kv, 2)), dma((2, kv, 2)), dma((2, kv, 2)),
            dma((n_tp - 1,)), dma((n_tp - 1,)), dma((2,)), dma((2,)),
            dma((n_hop,)), dma((n_flow, n_hop)), dma((n_flow, n_hop)),
        ],
        compiler_params=pltpu.CompilerParams(collective_id=0, has_side_effects=True),
    )(
        block_adapter_choice, normed_input.T, query, key, value,
        adapter_down_maps, adapter_up_maps,
    )


def solution(mesh):
    placed = (
        P("seq", "tp"),
        P("seq", "tp"),
        P("seq", "tp"),
        P("seq", "tp"),
        P(None, None, "tp"),
        P(None, None, "tp"),
        P(),
    )
    return jax.shard_map(
        functools.partial(on_device, mesh.shape["seq"], mesh.shape["tp"]),
        mesh=mesh, in_specs=placed, out_specs=P("seq", "tp"), check_vma=False,
    )
```
